256 devices in a mesh: dp: 4 (over x), expert: 64 (over z, y, core).
Axes of the slice: x: 4, y: 4, z: 8, core: 2. Of those that a mesh axis runs over, the one named last changes fastest.
Arguments:
- expert_ids: int32 [12288, 8], P(('dp', 'expert')), may hold values from 0 to 63, all different within a row; in each aligned block of 48 rows (0 to 47, 48 to 95, ...) at most 9 rows name the same one
- route_probs: float32 [12288, 8], P(('dp', 'expert')), may hold values from 0.02 to 0.5
- expert_hidden: bfloat16 [4, 64, 64, 9, 768], P('dp', 'expert'), may hold values from -6 to 6
- down_weight: bfloat16 [64, 768, 4096], P('expert', None, 'dp'), may hold values from -0.21875 to 0.21875
- out_grad: bfloat16 [12288, 4096], P(('dp', 'expert')), may hold values from -0.75 to 0.75
Outputs:
- layer_out: bfloat16 [12288, 4096], P(('dp', 'expert'))
- prob_grad: float32 [12288, 8], P(('dp', 'expert'))
- hidden_grad: bfloat16 [4, 64, 64, 9, 768], P('dp', 'expert')
- weight_grad: float32 [64, 768, 4096], P('expert', None, 'dp')
The draws below stay inside these ranges and needn't reach their ends.
Inputs may be any that keep to these rules, and one draw needn't show every extreme that they name: `expert_ids`: each row names 8 different experts. Among the rows of one device no expert is named by more than 9 rows, and in every draw some device names some expert exactly 9 times.
All inputs are finite; a program needn't handle non-finite values.
Results may differ from the reference program's by a relative error of at most 0.0085.
Values may be sent and summed in bfloat16 or wider, within the bound.
A program may use at most 128 MiB of HBM per device.

```python
import math
import jax
import jax.numpy as jnp
import numpy as np
from jax import lax

D = 4096
FF = 768
TOP = 8
TOK_DEV = 48
EXPERTS = 64
CAP = 9
TOKENS = 12288
N_DP = 4
N_EXPERT = 64


def levels(rng, dims, split, low, top_value):
    gain = 1.0
    for dim, blocks in split:
        heights = jax.random.uniform(jax.random.fold_in(jax.random.fold_in(rng, 6), dim), (blocks,), jnp.float32, low / len(split), top_value / len(split))
        gain = gain * jnp.repeat(jnp.exp(heights), dims[dim] // blocks).reshape((-1,) + (1,) * (len(dims) - 1 - dim))
    return gain


def shared_out(stream_key, own, number, rows, amount, top, most, lean):
    order = jax.random.permutation(stream_key, amount)
    packed, common = portions_of(amount, rows * top, most, lean, True), portions_of(amount, rows * top, most, lean, False)
    places = jnp.arange(amount)

    def named(sizes, offset_by):
        used = int((sizes > 0).sum())
        fixed = max(1, used // 4)
        passed = fixed + (places - fixed + offset_by * (used - fixed)) % max(1, amount - fixed)
        return jnp.zeros((amount,), jnp.int32).at[order[jnp.where(places < fixed, places, passed)]].set(jnp.asarray(sizes, jnp.int32))

    sizes = jnp.where(number % 4 == 0, named(packed, number // 4), named(common, number - number // 4 - 1))
    mixed = jax.random.permutation(jax.random.fold_in(own, 3), amount)
    giver, taker = mixed[0:amount // 2 * 2:2], mixed[1:amount // 2 * 2:2]
    room = jnp.minimum(sizes[giver] - 1, most - sizes[taker]) // 2
    room = jnp.where((giver == order[0]) | (taker == order[0]) | (sizes[taker] == 0), 0, jnp.maximum(room, 0))
    passed = jax.random.randint(jax.random.fold_in(own, 4), (amount // 2,), 0, 1 << 20) % (room + 1)
    sizes = sizes.at[giver].add(-passed).at[taker].add(passed)
    labels = jnp.searchsorted(jnp.cumsum(sizes), jnp.arange(rows * top), side="right").astype(jnp.int32)
    grid = labels.reshape(top, rows).T
    grid = grid[jax.random.permutation(jax.random.fold_in(own, 1), rows)]
    offset_by = jax.random.randint(jax.random.fold_in(own, 2), (rows, 1), 0, top)
    return jnp.take_along_axis(grid, (jnp.arange(top)[None, :] + offset_by) % top, axis=1)


def portions_of(count, total, reach, skew, full):
    weights = [(1 << 20) // math.isqrt(rank ** skew) + 1 for rank in range(1, count + 1)]
    largest = reach if full else min(reach, max(-(-total // count), total * weights[0] // sum(weights)))
    least = 1 if total - largest >= count - 1 else 0
    counts, surplus = [largest] + [least] * (count - 1), total - largest - least * (count - 1)
    while surplus > 0:
        free = [i for i in range(1, count) if counts[i] < largest] or [i for i in range(1, count) if counts[i] < reach]
        pool, budget = sum([weights[i] for i in free]), surplus
        for i in free:
            extra = min(reach - counts[i], max(1, budget * weights[i] // pool), surplus)
            counts[i] = counts[i] + extra
            surplus = surplus - extra
    return np.array(counts)


def gaussian(stream_key, extent, width, reach, split=(), kind=jnp.bfloat16):
    result = jax.random.normal(stream_key, extent, jnp.float32) * width
    if len(split) > 0:
        result = levels(stream_key, extent, split, -0.22, 0.18) * result
    return jnp.clip(result, min=-reach, max=reach).astype(kind)


def setup_inputs(seed: int = 0) -> dict:
    seeds = jax.random.split(jax.random.key(seed), 6)
    expert_ids_keys = jax.random.split(jax.random.fold_in(seeds[0], 1), TOKENS // TOK_DEV)
    expert_ids_turns = jax.random.permutation(jax.random.fold_in(seeds[0], 3), TOKENS // TOK_DEV)
    expert_ids = jax.vmap(lambda own, number: shared_out(jax.random.fold_in(seeds[0], 2), own, number, TOK_DEV, EXPERTS, TOP, CAP, 1))(expert_ids_keys, expert_ids_turns).reshape((TOKENS, TOP))
    route_probs = jnp.clip(jnp.exp(math.log(0.5) - 3.218876 * jax.random.uniform(seeds[1], (TOKENS, TOP), jnp.float32) ** levels(seeds[1], (TOKENS, TOP), ((0, 256),), -0.2, 0.2)), 0.02, 0.5)
    expert_hidden = gaussian(seeds[2], (N_DP, EXPERTS, N_EXPERT, CAP, FF), 1.0, 6.0, ((0, 4), (1, 64)))
    down_weight = gaussian(seeds[3], (EXPERTS, FF, D), FF ** -0.5, 0.21875, ((0, 64), (2, 4)))
    out_grad = gaussian(seeds[4], (TOKENS, D), 0.125, 0.75, ((0, 256),))
    return {"expert_ids": expert_ids, "route_probs": route_probs, "expert_hidden": expert_hidden, "down_weight": down_weight, "out_grad": out_grad}


def reference(expert_ids, route_probs, expert_hidden, down_weight, out_grad):
    blocks = N_DP * N_EXPERT
    routes = TOK_DEV * TOP
    route_ids = expert_ids.reshape(blocks, routes).astype(jnp.int32)
    onehot = (route_ids[:, :, None] == jnp.arange(EXPERTS, dtype=jnp.int32)[None, None, :]).astype(jnp.int32)
    earlier = jnp.cumsum(onehot, axis=1) - onehot
    position = jnp.sum(earlier * onehot, axis=2).astype(jnp.int32)
    block_index = jnp.broadcast_to(jnp.arange(blocks, dtype=jnp.int32)[:, None], (blocks, routes))
    route_index = jnp.broadcast_to(jnp.arange(routes, dtype=jnp.int32)[None, :], (blocks, routes))
    slot_route = jnp.full((blocks, EXPERTS, CAP), -1, dtype=jnp.int32)
    slot_route = slot_route.at[block_index, route_ids, position].set(route_index)
    slot_route = slot_route.reshape(N_DP, N_EXPERT, EXPERTS, CAP).transpose(0, 2, 1, 3)
    probs_blocks = route_probs.reshape(N_DP, N_EXPERT, routes)
    grads_blocks = out_grad.reshape(N_DP, N_EXPERT, TOK_DEV, D)
    sources = jnp.arange(N_EXPERT, dtype=jnp.int32)[:, None]

    def step(carry, expert):
        layer_acc, prob_acc = carry
        weight = lax.dynamic_index_in_dim(down_weight, expert, 0, keepdims=False)
        grads_out = []
        weight_sum = jnp.zeros((FF, D), jnp.float32)
        for replica in range(N_DP):
            owners = lax.dynamic_index_in_dim(slot_route[replica], expert, 0, keepdims=False)
            filled = owners >= 0
            safe_owner = jnp.maximum(owners, 0)
            slot_token = safe_owner // TOP
            hidden_rows = lax.dynamic_index_in_dim(expert_hidden[replica], expert, 0, keepdims=False).reshape(N_EXPERT * CAP, FF)
            slot_out = jnp.dot(hidden_rows, weight, preferred_element_type=jnp.float32).astype(jnp.bfloat16)
            slot_cube = slot_out.reshape(N_EXPERT, CAP, D).astype(jnp.float32)
            slot_prob = jnp.where(filled, probs_blocks[replica][sources, safe_owner], jnp.float32(0.0))
            slot_cot = grads_blocks[replica][sources, slot_token].astype(jnp.float32)
            layer_acc = layer_acc.at[replica, sources, slot_token].add(slot_prob[:, :, None] * slot_cube)
            inner = jnp.sum(slot_cot * slot_cube, axis=2)
            prob_acc = prob_acc.at[replica, sources, safe_owner].add(jnp.where(filled, inner, jnp.float32(0.0)))
            scaled = (slot_prob[:, :, None] * slot_cot).astype(jnp.bfloat16).reshape(N_EXPERT * CAP, D)
            back = jnp.dot(scaled, weight.T, preferred_element_type=jnp.float32).astype(jnp.bfloat16)
            grads_out.append(back.reshape(N_EXPERT, CAP, FF))
            partial_value = jnp.dot(hidden_rows.T, scaled, preferred_element_type=jnp.float32).astype(jnp.bfloat16)
            weight_sum = weight_sum + partial_value.astype(jnp.float32)
        return (layer_acc, prob_acc), (jnp.stack(grads_out), weight_sum)

    start = (jnp.zeros((N_DP, N_EXPERT, TOK_DEV, D), jnp.float32), jnp.zeros((N_DP, N_EXPERT, routes), jnp.float32))
    (layer_acc, prob_acc), (grads_all, weight_grad) = lax.scan(step, start, jnp.arange(EXPERTS, dtype=jnp.int32))
    layer_out = layer_acc.reshape(TOKENS, D).astype(jnp.bfloat16)
    prob_grad = prob_acc.reshape(TOKENS, TOP)
    hidden_grad = grads_all.transpose(1, 0, 2, 3, 4)
    return layer_out, prob_grad, hidden_grad, weight_grad
```

```python
import jax
import jax.numpy as jnp
from jax import lax
from jax.sharding import PartitionSpec as P


def rounded_partial(values):
    narrow = lax.optimization_barrier(values.astype(jnp.bfloat16))
    return narrow.astype(jnp.float32)


def shards(expert_ids, route_probs, expert_hidden, down_weight, out_grad):
    tok_count, top_count = expert_ids.shape
    expert_count = lax.axis_size("expert")
    capacity = expert_hidden.shape[3]
    hidden_width = down_weight.shape[1]
    model_width = out_grad.shape[1]
    slot_count = expert_count * capacity
    flat_ids = expert_ids.reshape(-1)
    onehot = (flat_ids[:, None] == jnp.arange(expert_count, dtype=jnp.int32)[None, :]).astype(
        jnp.int32
    )
    earlier = jnp.cumsum(onehot, axis=0) - onehot
    position = jnp.sum(earlier * onehot, axis=1)
    slot_index = flat_ids * capacity + position
    slot_owner = (
        jnp.full((slot_count,), -1, dtype=jnp.int32)
        .at[slot_index]
        .set(jnp.arange(tok_count * top_count, dtype=jnp.int32))
    )
    filled = slot_owner >= 0
    safe_owner = jnp.maximum(slot_owner, 0)
    hidden_rows = expert_hidden.reshape(-1, hidden_width)
    flat_probs = route_probs.reshape(-1)
    slot_prob = jnp.where(filled, flat_probs[safe_owner], jnp.float32(0.0))
    slot_out = jnp.dot(
        hidden_rows,
        lax.all_gather(down_weight, "dp", axis=2, tiled=True)[0],
        preferred_element_type=jnp.float32,
    ).astype(jnp.bfloat16)
    returned = lax.all_to_all(
        slot_out.reshape(expert_count, capacity, model_width // 128, 128),
        "expert",
        split_axis=0,
        concat_axis=0,
        tiled=True,
    )
    route_out = returned.reshape(slot_count, model_width)[slot_index].reshape(
        tok_count, top_count, model_width
    )
    layer_out = jnp.einsum(
        "tk,tkd->td", route_probs, route_out, preferred_element_type=jnp.float32
    ).astype(jnp.bfloat16)
    prob_grad = jnp.einsum("td,tkd->tk", out_grad, route_out, preferred_element_type=jnp.float32)
    scaled = (slot_prob[:, None] * out_grad[safe_owner // top_count]).astype(jnp.bfloat16)
    arrived = lax.all_to_all(
        scaled.reshape(expert_count, capacity, model_width // 128, 128),
        "expert",
        split_axis=0,
        concat_axis=0,
        tiled=True,
    )
    arrived = arrived.reshape(-1, model_width)
    partial_value = jnp.einsum(
        "rf,rd->fd", hidden_rows, arrived, preferred_element_type=jnp.float32
    )[None]
    weight_grad = lax.psum_scatter(
        rounded_partial(partial_value).astype(jnp.bfloat16), "dp", scatter_dimension=2, tiled=True
    ).astype(jnp.float32)
    hidden_total = jnp.einsum(
        "rd,fd->rf",
        arrived,
        lax.all_gather(down_weight, "dp", axis=2, tiled=True)[0],
        preferred_element_type=jnp.float32,
    )
    hidden_grad = hidden_total.astype(jnp.bfloat16).reshape(expert_hidden.shape)
    return (layer_out, prob_grad, hidden_grad, weight_grad)


def solution(mesh):
    placed = (
        P(("dp", "expert"), None),
        P(("dp", "expert"), None),
        P("dp", "expert", None, None, None),
        P("expert", None, "dp"),
        P(("dp", "expert"), None),
    )
    return jax.shard_map(
        shards,
        mesh=mesh,
        in_specs=placed,
        out_specs=(
            P(("dp", "expert"), None),
            P(("dp", "expert"), None),
            P("dp", "expert", None, None, None),
            P("expert", None, "dp"),
        ),
        check_vma=False,
    )
```

```python
import functools

import jax
import jax.numpy as jnp
from jax import lax
from jax.experimental import pallas as pl
from jax.experimental.pallas import tpu as pltpu
from jax.sharding import PartitionSpec as P

MESH = pl.DeviceIdType.MESH


def exchange_kernel(n, fwd_in, bwd_in, fwd_out, bwd_out, send_sem, recv_sem, own_sem):
    me = lax.axis_index("expert")
    row = lax.axis_index("dp")
    pairs = ((fwd_in, fwd_out), (bwd_in, bwd_out))

    barrier = pltpu.get_barrier_semaphore()

    def greet(i, carry):
        peer = lax.rem(me + i, n)
        pl.semaphore_signal(barrier, inc=1, device_id=(row, peer), device_id_type=MESH)
        return carry

    lax.fori_loop(1, n, greet, 0)
    pl.semaphore_wait(barrier, n - 1)

    own = [
        pltpu.make_async_copy(src.at[me], dst.at[me], own_sem.at[a])
        for a, (src, dst) in enumerate(pairs)
    ]
    for copy in own:
        copy.start()

    def remote(a, peer, source):
        src, dst = pairs[a]
        return pltpu.make_async_remote_copy(
            src_ref=src.at[peer],
            dst_ref=dst.at[source],
            send_sem=send_sem.at[a, peer],
            recv_sem=recv_sem.at[a, source],
            device_id=(row, peer),
            device_id_type=MESH,
        )

    def start(i, carry):
        peer = lax.rem(me + i, n)
        for a in range(2):
            remote(a, peer, me).start()
        return carry

    lax.fori_loop(1, n, start, 0)

    def finish(i, carry):
        peer = lax.rem(me + i, n)
        source = lax.rem(me + n - i, n)
        for a in range(2):
            remote(a, peer, me).wait_send()
            remote(a, source, source).wait_recv()
        return carry

    lax.fori_loop(1, n, finish, 0)
    for copy in own:
        copy.wait()


def exchange(fwd, bwd):
    n = lax.axis_size("expert")
    any_spec = pl.BlockSpec(memory_space=pl.ANY)
    return pl.pallas_call(
        functools.partial(exchange_kernel, n),
        out_shape=(
            jax.ShapeDtypeStruct(fwd.shape, fwd.dtype),
            jax.ShapeDtypeStruct(bwd.shape, bwd.dtype),
        ),
        in_specs=[any_spec, any_spec],
        out_specs=(any_spec, any_spec),
        scratch_shapes=[
            pltpu.SemaphoreType.DMA((2, n)),
            pltpu.SemaphoreType.DMA((2, n)),
            pltpu.SemaphoreType.DMA((2,)),
        ],
        compiler_params=pltpu.CompilerParams(collective_id=0, has_side_effects=True),
    )(fwd, bwd)


def rounded_partial(values):
    narrow = lax.optimization_barrier(values.astype(jnp.bfloat16))
    return narrow.astype(jnp.float32)


def shards(expert_ids, route_probs, expert_hidden, down_weight, out_grad):
    tok_count, top_count = expert_ids.shape
    expert_count = lax.axis_size("expert")
    capacity = expert_hidden.shape[3]
    hidden_width = down_weight.shape[1]
    model_width = out_grad.shape[1]
    slot_count = expert_count * capacity
    flat_ids = expert_ids.reshape(-1)
    onehot = (flat_ids[:, None] == jnp.arange(expert_count, dtype=jnp.int32)[None, :]).astype(
        jnp.int32
    )
    earlier = jnp.cumsum(onehot, axis=0) - onehot
    position = jnp.sum(earlier * onehot, axis=1)
    slot_index = flat_ids * capacity + position
    slot_owner = (
        jnp.full((slot_count,), -1, dtype=jnp.int32)
        .at[slot_index]
        .set(jnp.arange(tok_count * top_count, dtype=jnp.int32))
    )
    filled = slot_owner >= 0
    safe_owner = jnp.maximum(slot_owner, 0)
    hidden_rows = expert_hidden.reshape(-1, hidden_width)
    flat_probs = route_probs.reshape(-1)
    slot_prob = jnp.where(filled, flat_probs[safe_owner], jnp.float32(0.0))
    slot_out = jnp.dot(
        hidden_rows,
        lax.all_gather(down_weight, "dp", axis=2, tiled=True)[0],
        preferred_element_type=jnp.float32,
    ).astype(jnp.bfloat16)
    scaled = (slot_prob[:, None] * out_grad[safe_owner // top_count]).astype(jnp.bfloat16)
    returned, arrived = exchange(
        slot_out.reshape(expert_count, capacity, model_width // 128, 128),
        scaled.reshape(expert_count, capacity, model_width // 128, 128),
    )
    route_out = returned.reshape(slot_count, model_width)[slot_index].reshape(
        tok_count, top_count, model_width
    )
    layer_out = jnp.einsum(
        "tk,tkd->td", route_probs, route_out, preferred_element_type=jnp.float32
    ).astype(jnp.bfloat16)
    prob_grad = jnp.einsum("td,tkd->tk", out_grad, route_out, preferred_element_type=jnp.float32)
    arrived = arrived.reshape(-1, model_width)
    partial_value = jnp.einsum(
        "rf,rd->fd", hidden_rows, arrived, preferred_element_type=jnp.float32
    )[None]
    weight_grad = lax.psum_scatter(
        rounded_partial(partial_value).astype(jnp.bfloat16), "dp", scatter_dimension=2, tiled=True
    ).astype(jnp.float32)
    hidden_total = jnp.einsum(
        "rd,fd->rf",
        arrived,
        lax.all_gather(down_weight, "dp", axis=2, tiled=True)[0],
        preferred_element_type=jnp.float32,
    )
    hidden_grad = hidden_total.astype(jnp.bfloat16).reshape(expert_hidden.shape)
    return (layer_out, prob_grad, hidden_grad, weight_grad)


def solution(mesh):
    placed = (
        P(("dp", "expert"), None),
        P(("dp", "expert"), None),
        P("dp", "expert", None, None, None),
        P("expert", None, "dp"),
        P(("dp", "expert"), None),
    )
    return jax.shard_map(
        shards,
        mesh=mesh,
        in_specs=placed,
        out_specs=(
            P(("dp", "expert"), None),
            P(("dp", "expert"), None),
            P("dp", "expert", None, None, None),
            P("expert", None, "dp"),
        ),
        check_vma=False,
    )
```

```python
import functools

import jax
import jax.numpy as jnp
from jax import lax
from jax.experimental import pallas as pl
from jax.experimental.pallas import tpu as pltpu
from jax.sharding import PartitionSpec as P

MESH = pl.DeviceIdType.MESH


def exchange_kernel(n, src, dst, send_sem, recv_sem, own_sem):
    me = lax.axis_index("expert")
    row = lax.axis_index("dp")

    barrier = pltpu.get_barrier_semaphore()

    def greet(i, carry):
        peer = lax.rem(me + i, n)
        pl.semaphore_signal(barrier, inc=1, device_id=(row, peer), device_id_type=MESH)
        return carry

    lax.fori_loop(1, n, greet, 0)
    pl.semaphore_wait(barrier, n - 1)

    own = pltpu.make_async_copy(src.at[me], dst.at[me], own_sem)
    own.start()

    def remote(peer, source):
        return pltpu.make_async_remote_copy(
            src_ref=src.at[peer],
            dst_ref=dst.at[source],
            send_sem=send_sem.at[peer],
            recv_sem=recv_sem.at[source],
            device_id=(row, peer),
            device_id_type=MESH,
        )

    def start(i, carry):
        remote(lax.rem(me + i, n), me).start()
        return carry

    lax.fori_loop(1, n, start, 0)

    def finish(i, carry):
        source = lax.rem(me + n - i, n)
        remote(lax.rem(me + i, n), me).wait_send()
        remote(source, source).wait_recv()
        return carry

    lax.fori_loop(1, n, finish, 0)
    own.wait()


def exchange(x, collective):
    n = lax.axis_size("expert")
    any_spec = pl.BlockSpec(memory_space=pl.ANY)
    return pl.pallas_call(
        functools.partial(exchange_kernel, n),
        out_shape=jax.ShapeDtypeStruct(x.shape, x.dtype),
        in_specs=[any_spec],
        out_specs=any_spec,
        scratch_shapes=[
            pltpu.SemaphoreType.DMA((n,)),
            pltpu.SemaphoreType.DMA((n,)),
            pltpu.SemaphoreType.DMA(()),
        ],
        compiler_params=pltpu.CompilerParams(collective_id=collective, has_side_effects=True),
    )(x)


def shards(expert_ids, route_probs, expert_hidden, down_weight, out_grad):
    tok_count, top_count = expert_ids.shape
    expert_count = lax.axis_size("expert")
    capacity = expert_hidden.shape[3]
    hidden_width = down_weight.shape[1]
    model_width = out_grad.shape[1]
    slot_count = expert_count * capacity
    flat_ids = expert_ids.reshape(-1)
    onehot = (flat_ids[:, None] == jnp.arange(expert_count, dtype=jnp.int32)[None, :]).astype(
        jnp.int32
    )
    earlier = jnp.cumsum(onehot, axis=0) - onehot
    position = jnp.sum(earlier * onehot, axis=1)
    slot_index = flat_ids * capacity + position
    slot_owner = (
        jnp.full((slot_count,), -1, dtype=jnp.int32)
        .at[slot_index]
        .set(jnp.arange(tok_count * top_count, dtype=jnp.int32))
    )
    filled = slot_owner >= 0
    safe_owner = jnp.maximum(slot_owner, 0)
    hidden_rows = expert_hidden.reshape(-1, hidden_width)
    flat_probs = route_probs.reshape(-1)
    slot_prob = jnp.where(filled, flat_probs[safe_owner], jnp.float32(0.0))
    scaled = (slot_prob[:, None] * out_grad[safe_owner // top_count]).astype(jnp.bfloat16)
    arrived = exchange(scaled.reshape(expert_count, capacity, model_width // 128, 128), 0)
    gathered_weight = lax.all_gather(down_weight, "dp", axis=2, tiled=True)[0]
    slot_out = jnp.dot(
        hidden_rows, gathered_weight, preferred_element_type=jnp.float32
    ).astype(jnp.bfloat16)
    arrived = arrived.reshape(-1, model_width)
    partial_value = jnp.einsum(
        "rf,rd->fd", hidden_rows, arrived, preferred_element_type=jnp.float32
    )[None]
    slot_out, narrow = lax.optimization_barrier((slot_out, partial_value.astype(jnp.bfloat16)))
    weight_grad = lax.psum_scatter(narrow, "dp", scatter_dimension=2, tiled=True).astype(
        jnp.float32
    )
    returned = exchange(slot_out.reshape(expert_count, capacity, model_width // 128, 128), 1)
    route_out = returned.reshape(slot_count, model_width)[slot_index].reshape(
        tok_count, top_count, model_width
    )
    layer_out = jnp.einsum(
        "tk,tkd->td", route_probs, route_out, preferred_element_type=jnp.float32
    ).astype(jnp.bfloat16)
    prob_grad = jnp.einsum("td,tkd->tk", out_grad, route_out, preferred_element_type=jnp.float32)
    hidden_total = jnp.einsum(
        "rd,fd->rf",
        arrived,
        gathered_weight,
        preferred_element_type=jnp.float32,
    )
    hidden_grad = hidden_total.astype(jnp.bfloat16).reshape(expert_hidden.shape)
    return (layer_out, prob_grad, hidden_grad, weight_grad)


def solution(mesh):
    placed = (
        P(("dp", "expert"), None),
        P(("dp", "expert"), None),
        P("dp", "expert", None, None, None),
        P("expert", None, "dp"),
        P(("dp", "expert"), None),
    )
    return jax.shard_map(
        shards,
        mesh=mesh,
        in_specs=placed,
        out_specs=(
            P(("dp", "expert"), None),
            P(("dp", "expert"), None),
            P("dp", "expert", None, None, None),
            P("expert", None, "dp"),
        ),
        check_vma=False,
    )
```

```python
import jax
import jax.numpy as jnp
from jax import lax
from jax.sharding import PartitionSpec as P


def rounded_partial(values):
    narrow = lax.optimization_barrier(values.astype(jnp.bfloat16))
    return narrow.astype(jnp.float32)


def shards(expert_ids, route_probs, expert_hidden, down_weight, out_grad):
    tok_count, top_count = expert_ids.shape
    expert_count = lax.axis_size("expert")
    capacity = expert_hidden.shape[3]
    hidden_width = down_weight.shape[1]
    model_width = out_grad.shape[1]
    slot_count = expert_count * capacity
    flat_ids = expert_ids.reshape(-1)
    onehot = (flat_ids[:, None] == jnp.arange(expert_count, dtype=jnp.int32)[None, :]).astype(
        jnp.int32
    )
    earlier = jnp.cumsum(onehot, axis=0) - onehot
    position = jnp.sum(earlier * onehot, axis=1)
    slot_index = flat_ids * capacity + position
    slot_owner = (
        jnp.full((slot_count,), -1, dtype=jnp.int32)
        .at[slot_index]
        .set(jnp.arange(tok_count * top_count, dtype=jnp.int32))
    )
    filled = slot_owner >= 0
    safe_owner = jnp.maximum(slot_owner, 0)
    hidden_rows = expert_hidden.reshape(-1, hidden_width)
    flat_probs = route_probs.reshape(-1)
    slot_prob = jnp.where(filled, flat_probs[safe_owner], jnp.float32(0.0))
    lanes = 128
    grad_tiles = out_grad.reshape(tok_count, model_width // lanes, lanes)
    gathered_weight = lax.all_gather(down_weight, "dp", axis=2, tiled=True)[0]
    slot_out = jnp.dot(
        hidden_rows, gathered_weight, preferred_element_type=jnp.float32
    ).astype(jnp.bfloat16)
    returned = lax.all_to_all(
        slot_out.reshape(expert_count, capacity, model_width // lanes, lanes),
        "expert",
        split_axis=0,
        concat_axis=0,
        tiled=True,
    )
    route_out = returned.reshape(slot_count, model_width // lanes, lanes)[slot_index].reshape(
        tok_count, top_count, model_width // lanes, lanes
    ).astype(jnp.float32)
    layer_out = jnp.sum(route_probs[:, :, None, None] * route_out, axis=1)
    layer_out = layer_out.astype(jnp.bfloat16).reshape(tok_count, model_width)
    prob_grad = jnp.sum(
        grad_tiles[:, None].astype(jnp.float32) * route_out, axis=(2, 3)
    )
    scaled = (
        slot_prob[:, None, None] * grad_tiles[safe_owner // top_count].astype(jnp.float32)
    ).astype(jnp.bfloat16)
    arrived = lax.all_to_all(
        scaled.reshape(expert_count, capacity, model_width // lanes, lanes),
        "expert",
        split_axis=0,
        concat_axis=0,
        tiled=True,
    )
    arrived = lax.optimization_barrier(arrived.reshape(-1, model_width))
    partial_value = jnp.einsum(
        "rf,rd->fd", hidden_rows, arrived, preferred_element_type=jnp.float32
    )[None]
    weight_grad = lax.psum_scatter(
        rounded_partial(partial_value).astype(jnp.bfloat16), "dp", scatter_dimension=2, tiled=True
    ).astype(jnp.float32)
    hidden_total = jnp.einsum(
        "rd,fd->rf", arrived, gathered_weight, preferred_element_type=jnp.float32
    )
    hidden_grad = hidden_total.astype(jnp.bfloat16).reshape(expert_hidden.shape)
    return (layer_out, prob_grad, hidden_grad, weight_grad)


def solution(mesh):
    placed = (
        P(("dp", "expert"), None),
        P(("dp", "expert"), None),
        P("dp", "expert", None, None, None),
        P("expert", None, "dp"),
        P(("dp", "expert"), None),
    )
    return jax.shard_map(
        shards,
        mesh=mesh,
        in_specs=placed,
        out_specs=(
            P(("dp", "expert"), None),
            P(("dp", "expert"), None),
            P("dp", "expert", None, None, None),
            P("expert", None, "dp"),
        ),
        check_vma=False,
    )
```

```python
import jax
import jax.numpy as jnp
from jax import lax
from jax.sharding import PartitionSpec as P


def rounded_partial(values):
    narrow = lax.optimization_barrier(values.astype(jnp.bfloat16))
    return narrow.astype(jnp.float32)


def shards(expert_ids, route_probs, expert_hidden, down_weight, out_grad):
    tok_count, top_count = expert_ids.shape
    expert_count = lax.axis_size("expert")
    capacity = expert_hidden.shape[3]
    hidden_width = down_weight.shape[1]
    model_width = out_grad.shape[1]
    slot_count = expert_count * capacity
    flat_ids = expert_ids.reshape(-1)
    onehot = (flat_ids[:, None] == jnp.arange(expert_count, dtype=jnp.int32)[None, :]).astype(
        jnp.int32
    )
    earlier = jnp.cumsum(onehot, axis=0) - onehot
    position = jnp.sum(earlier * onehot, axis=1)
    slot_index = flat_ids * capacity + position
    slot_owner = (
        jnp.full((slot_count,), -1, dtype=jnp.int32)
        .at[slot_index]
        .set(jnp.arange(tok_count * top_count, dtype=jnp.int32))
    )
    filled = slot_owner >= 0
    safe_owner = jnp.maximum(slot_owner, 0)
    hidden_rows = expert_hidden.reshape(-1, hidden_width)
    flat_probs = route_probs.reshape(-1)
    slot_prob = jnp.where(filled, flat_probs[safe_owner], jnp.float32(0.0))
    lanes = 128
    grad_tiles = out_grad.reshape(tok_count, model_width // lanes, lanes)
    gathered_weight = lax.all_gather(down_weight, "dp", axis=2, tiled=True)[0]
    halves = 2
    tiles = model_width // lanes // halves
    width = tiles * lanes

    def swap(x):
        return lax.all_to_all(
            x.reshape(expert_count, capacity, tiles, lanes),
            "expert",
            split_axis=0,
            concat_axis=0,
            tiled=True,
        )

    layer_parts, prob_parts, weight_parts, hidden_parts = [], [], [], []
    arrived_parts = []
    for h in range(halves):
        scaled = (
            slot_prob[:, None, None]
            * grad_tiles[safe_owner // top_count, h * tiles : (h + 1) * tiles].astype(jnp.float32)
        ).astype(jnp.bfloat16)
        arrived_parts.append(swap(scaled))
    for h in range(halves):
        weight_half = gathered_weight[:, h * width : (h + 1) * width]
        slot_out = jnp.dot(hidden_rows, weight_half, preferred_element_type=jnp.float32).astype(
            jnp.bfloat16
        )
        returned = swap(slot_out)
        route_out = returned.reshape(slot_count, tiles, lanes)[slot_index].reshape(
            tok_count, top_count, tiles, lanes
        ).astype(jnp.float32)
        layer_parts.append(jnp.sum(route_probs[:, :, None, None] * route_out, axis=1))
        prob_parts.append(
            jnp.sum(
                grad_tiles[:, None, h * tiles : (h + 1) * tiles].astype(jnp.float32) * route_out,
                axis=(2, 3),
            )
        )
        arrived = arrived_parts[h].reshape(-1, width)
        weight_parts.append(
            jnp.einsum("rf,rd->fd", hidden_rows, arrived, preferred_element_type=jnp.float32)
        )
        hidden_parts.append(
            jnp.einsum("rd,fd->rf", arrived, weight_half, preferred_element_type=jnp.float32)
        )
    layer_out = jnp.concatenate(layer_parts, axis=1).astype(jnp.bfloat16)
    layer_out = layer_out.reshape(tok_count, model_width)
    prob_grad = prob_parts[0] + prob_parts[1]
    partial_value = jnp.concatenate(weight_parts, axis=1)[None]
    weight_grad = lax.psum_scatter(
        rounded_partial(partial_value).astype(jnp.bfloat16), "dp", scatter_dimension=2, tiled=True
    ).astype(jnp.float32)
    hidden_total = hidden_parts[0] + hidden_parts[1]
    hidden_grad = hidden_total.astype(jnp.bfloat16).reshape(expert_hidden.shape)
    return (layer_out, prob_grad, hidden_grad, weight_grad)


def solution(mesh):
    placed = (
        P(("dp", "expert"), None),
        P(("dp", "expert"), None),
        P("dp", "expert", None, None, None),
        P("expert", None, "dp"),
        P(("dp", "expert"), None),
    )
    return jax.shard_map(
        shards,
        mesh=mesh,
        in_specs=placed,
        out_specs=(
            P(("dp", "expert"), None),
            P(("dp", "expert"), None),
            P("dp", "expert", None, None, None),
            P("expert", None, "dp"),
        ),
        check_vma=False,
    )
```

```python
import functools

import jax
import jax.numpy as jnp
from jax import lax
from jax.experimental import pallas as pl
from jax.experimental.pallas import tpu as pltpu
from jax.sharding import PartitionSpec as P

MESH = pl.DeviceIdType.MESH


def exchange_kernel(n, src, dst, send_sem, recv_sem, own_sem):
    me = lax.axis_index("expert")
    row = lax.axis_index("dp")

    barrier = pltpu.get_barrier_semaphore()

    def greet(i, carry):
        peer = lax.rem(me + i, n)
        pl.semaphore_signal(barrier, inc=1, device_id=(row, peer), device_id_type=MESH)
        return carry

    lax.fori_loop(1, n, greet, 0)
    pl.semaphore_wait(barrier, n - 1)

    own = pltpu.make_async_copy(src.at[me], dst.at[me], own_sem)
    own.start()

    def remote(peer, source):
        return pltpu.make_async_remote_copy(
            src_ref=src.at[peer],
            dst_ref=dst.at[source],
            send_sem=send_sem.at[peer],
            recv_sem=recv_sem.at[source],
            device_id=(row, peer),
            device_id_type=MESH,
        )

    def offset(i):
        odd = i % 2
        return odd * ((i + 1) // 2) + (1 - odd) * (n - i // 2)

    def start(i, carry):
        remote(lax.rem(me + offset(i), n), me).start()
        return carry

    lax.fori_loop(1, n, start, 0)

    def finish(i, carry):
        source = lax.rem(me + n - offset(i), n)
        remote(lax.rem(me + offset(i), n), me).wait_send()
        remote(source, source).wait_recv()
        return carry

    lax.fori_loop(1, n, finish, 0)
    own.wait()


def exchange(x, collective):
    n = lax.axis_size("expert")
    any_spec = pl.BlockSpec(memory_space=pl.ANY)
    return pl.pallas_call(
        functools.partial(exchange_kernel, n),
        out_shape=jax.ShapeDtypeStruct(x.shape, x.dtype),
        in_specs=[any_spec],
        out_specs=any_spec,
        scratch_shapes=[
            pltpu.SemaphoreType.DMA((n,)),
            pltpu.SemaphoreType.DMA((n,)),
            pltpu.SemaphoreType.DMA(()),
        ],
        compiler_params=pltpu.CompilerParams(collective_id=collective, has_side_effects=True),
    )(x)


def shards(expert_ids, route_probs, expert_hidden, down_weight, out_grad):
    tok_count, top_count = expert_ids.shape
    expert_count = lax.axis_size("expert")
    capacity = expert_hidden.shape[3]
    hidden_width = down_weight.shape[1]
    model_width = out_grad.shape[1]
    slot_count = expert_count * capacity
    flat_ids = expert_ids.reshape(-1)
    onehot = (flat_ids[:, None] == jnp.arange(expert_count, dtype=jnp.int32)[None, :]).astype(
        jnp.int32
    )
    earlier = jnp.cumsum(onehot, axis=0) - onehot
    position = jnp.sum(earlier * onehot, axis=1)
    slot_index = flat_ids * capacity + position
    slot_owner = (
        jnp.full((slot_count,), -1, dtype=jnp.int32)
        .at[slot_index]
        .set(jnp.arange(tok_count * top_count, dtype=jnp.int32))
    )
    filled = slot_owner >= 0
    safe_owner = jnp.maximum(slot_owner, 0)
    hidden_rows = expert_hidden.reshape(-1, hidden_width)
    flat_probs = route_probs.reshape(-1)
    slot_prob = jnp.where(filled, flat_probs[safe_owner], jnp.float32(0.0))
    lanes = 128
    grad_tiles = out_grad.reshape(tok_count, model_width // lanes, lanes)
    scaled = (
        slot_prob[:, None, None] * grad_tiles[safe_owner // top_count].astype(jnp.float32)
    ).astype(jnp.bfloat16)
    arrived = exchange(scaled.reshape(expert_count, capacity, model_width // lanes, lanes), 0)
    gathered_weight = lax.all_gather(down_weight, "dp", axis=2, tiled=True)[0]
    slot_out = jnp.dot(
        hidden_rows, gathered_weight, preferred_element_type=jnp.float32
    ).astype(jnp.bfloat16)
    arrived = arrived.reshape(-1, model_width)
    partial_value = jnp.einsum(
        "rf,rd->fd", hidden_rows, arrived, preferred_element_type=jnp.float32
    )[None]
    slot_out, narrow = lax.optimization_barrier((slot_out, partial_value.astype(jnp.bfloat16)))
    weight_grad = lax.psum_scatter(narrow, "dp", scatter_dimension=2, tiled=True).astype(
        jnp.float32
    )
    returned = exchange(slot_out.reshape(expert_count, capacity, model_width // lanes, lanes), 1)
    route_out = returned.reshape(slot_count, model_width // lanes, lanes)[slot_index].reshape(
        tok_count, top_count, model_width // lanes, lanes
    ).astype(jnp.float32)
    layer_out = jnp.sum(route_probs[:, :, None, None] * route_out, axis=1)
    layer_out = layer_out.astype(jnp.bfloat16).reshape(tok_count, model_width)
    prob_grad = jnp.sum(
        grad_tiles[:, None].astype(jnp.float32) * route_out, axis=(2, 3)
    )
    hidden_total = jnp.einsum(
        "rd,fd->rf", arrived, gathered_weight, preferred_element_type=jnp.float32
    )
    hidden_grad = hidden_total.astype(jnp.bfloat16).reshape(expert_hidden.shape)
    return (layer_out, prob_grad, hidden_grad, weight_grad)


def solution(mesh):
    placed = (
        P(("dp", "expert"), None),
        P(("dp", "expert"), None),
        P("dp", "expert", None, None, None),
        P("expert", None, "dp"),
        P(("dp", "expert"), None),
    )
    return jax.shard_map(
        shards,
        mesh=mesh,
        in_specs=placed,
        out_specs=(
            P(("dp", "expert"), None),
            P(("dp", "expert"), None),
            P("dp", "expert", None, None, None),
            P("expert", None, "dp"),
        ),
        check_vma=False,
    )
```

```python
import jax
import jax.numpy as jnp
from jax import lax
from jax.sharding import PartitionSpec as P


def rounded_partial(values):
    narrow = lax.optimization_barrier(values.astype(jnp.bfloat16))
    return narrow.astype(jnp.float32)


def shards(expert_ids, route_probs, expert_hidden, down_weight, out_grad):
    tok_count, top_count = expert_ids.shape
    expert_count = lax.axis_size("expert")
    capacity = expert_hidden.shape[3]
    hidden_width = down_weight.shape[1]
    model_width = out_grad.shape[1]
    slot_count = expert_count * capacity
    flat_ids = expert_ids.reshape(-1)
    onehot = (flat_ids[:, None] == jnp.arange(expert_count, dtype=jnp.int32)[None, :]).astype(
        jnp.int32
    )
    earlier = jnp.cumsum(onehot, axis=0) - onehot
    position = jnp.sum(earlier * onehot, axis=1)
    slot_index = flat_ids * capacity + position
    holds = slot_index[None, :] == jnp.arange(slot_count, dtype=jnp.int32)[:, None]
    route_token = jnp.arange(tok_count * top_count, dtype=jnp.int32) // top_count
    slot_token = jnp.sum(jnp.where(holds, route_token[None, :], 0), axis=1)
    slot_prob = jnp.sum(jnp.where(holds, route_probs.reshape(-1)[None, :], jnp.float32(0.0)), axis=1)
    hidden_rows = expert_hidden.reshape(-1, hidden_width)
    lanes = 128
    grad_tiles = out_grad.reshape(tok_count, model_width // lanes, lanes)
    gathered_weight = lax.all_gather(down_weight, "dp", axis=2, tiled=True)[0]
    slot_out = jnp.dot(
        hidden_rows, gathered_weight, preferred_element_type=jnp.float32
    ).astype(jnp.bfloat16)
    outgoing = slot_out.reshape(expert_count, capacity, model_width // lanes, lanes)
    returned = lax.all_to_all(
        outgoing,
        "expert",
        split_axis=0,
        concat_axis=0,
        tiled=True,
    )
    route_out = returned.reshape(slot_count, model_width // lanes, lanes)[slot_index].reshape(
        tok_count, top_count, model_width // lanes, lanes
    ).astype(jnp.float32)
    layer_out = jnp.sum(route_probs[:, :, None, None] * route_out, axis=1)
    layer_out = layer_out.astype(jnp.bfloat16).reshape(tok_count, model_width)
    prob_grad = jnp.sum(
        grad_tiles[:, None].astype(jnp.float32) * route_out, axis=(2, 3)
    )
    scaled = (
        slot_prob[:, None, None] * grad_tiles[slot_token].astype(jnp.float32)
    ).astype(jnp.bfloat16)
    arrived = lax.all_to_all(
        scaled.reshape(expert_count, capacity, model_width // lanes, lanes),
        "expert",
        split_axis=0,
        concat_axis=0,
        tiled=True,
    )
    arrived, _ = lax.optimization_barrier((arrived, outgoing))
    arrived = arrived.reshape(-1, model_width)
    partial_value = jnp.einsum(
        "rf,rd->fd", hidden_rows, arrived, preferred_element_type=jnp.float32
    )[None]
    weight_grad = lax.psum_scatter(
        rounded_partial(partial_value).astype(jnp.bfloat16), "dp", scatter_dimension=2, tiled=True
    ).astype(jnp.float32)
    hidden_total = jnp.einsum(
        "rd,fd->rf", arrived, gathered_weight, preferred_element_type=jnp.float32
    )
    hidden_grad = hidden_total.astype(jnp.bfloat16).reshape(expert_hidden.shape)
    return (layer_out, prob_grad, hidden_grad, weight_grad)


def solution(mesh):
    placed = (
        P(("dp", "expert"), None),
        P(("dp", "expert"), None),
        P("dp", "expert", None, None, None),
        P("expert", None, "dp"),
        P(("dp", "expert"), None),
    )
    return jax.shard_map(
        shards,
        mesh=mesh,
        in_specs=placed,
        out_specs=(
            P(("dp", "expert"), None),
            P(("dp", "expert"), None),
            P("dp", "expert", None, None, None),
            P("expert", None, "dp"),
        ),
        check_vma=False,
    )
```

```python
import jax
import jax.numpy as jnp
from jax import lax
from jax.sharding import PartitionSpec as P


def rounded_partial(values):
    narrow = lax.optimization_barrier(values.astype(jnp.bfloat16))
    return narrow.astype(jnp.float32)


def shards(expert_ids, route_probs, expert_hidden, down_weight, out_grad):
    tok_count, top_count = expert_ids.shape
    expert_count = lax.axis_size("expert")
    capacity = expert_hidden.shape[3]
    hidden_width = down_weight.shape[1]
    model_width = out_grad.shape[1]
    slot_count = expert_count * capacity
    flat_ids = expert_ids.reshape(-1)
    onehot = (flat_ids[:, None] == jnp.arange(expert_count, dtype=jnp.int32)[None, :]).astype(
        jnp.int32
    )
    earlier = jnp.cumsum(onehot, axis=0) - onehot
    position = jnp.sum(earlier * onehot, axis=1)
    slot_index = flat_ids * capacity + position
    holds = slot_index[None, :] == jnp.arange(slot_count, dtype=jnp.int32)[:, None]
    route_token = jnp.arange(tok_count * top_count, dtype=jnp.int32) // top_count
    slot_token = jnp.sum(jnp.where(holds, route_token[None, :], 0), axis=1)
    slot_prob = jnp.sum(jnp.where(holds, route_probs.reshape(-1)[None, :], jnp.float32(0.0)), axis=1)
    hidden_rows = expert_hidden.reshape(-1, hidden_width)
    lanes = 128
    grad_tiles = out_grad.reshape(tok_count, model_width // lanes, lanes)
    gathered_weight = lax.all_gather(down_weight, "dp", axis=2, tiled=True)[0]
    slot_out = jnp.dot(
        hidden_rows, gathered_weight, preferred_element_type=jnp.float32
    ).astype(jnp.bfloat16)
    outgoing = slot_out.reshape(expert_count, capacity, model_width // lanes, lanes)
    returned = lax.all_to_all(
        outgoing,
        "expert",
        split_axis=0,
        concat_axis=0,
        tiled=True,
    )
    route_out = returned.reshape(slot_count, model_width // lanes, lanes)[slot_index].reshape(
        tok_count, top_count, model_width // lanes, lanes
    ).astype(jnp.float32)
    layer_out = jnp.sum(route_probs[:, :, None, None] * route_out, axis=1)
    layer_out = layer_out.astype(jnp.bfloat16).reshape(tok_count, model_width)
    prob_grad = jnp.sum(
        grad_tiles[:, None].astype(jnp.float32) * route_out, axis=(2, 3)
    )
    scaled = (
        slot_prob[:, None, None] * grad_tiles[slot_token].astype(jnp.float32)
    ).astype(jnp.bfloat16)
    arrived = lax.all_to_all(
        scaled.reshape(expert_count, capacity, model_width // lanes, lanes),
        "expert",
        split_axis=0,
        concat_axis=0,
        tiled=True,
    )
    arrived, _ = lax.optimization_barrier((arrived, outgoing))
    arrived = arrived.reshape(-1, model_width)
    shard_count = lax.axis_size("dp")
    quarter = model_width // shard_count
    by_quarter = arrived.reshape(slot_count, shard_count, 2, quarter // 2)
    weight_parts = []
    for part in range(2):
        partial_value = jnp.einsum(
            "rf,rqd->fqd", hidden_rows, by_quarter[:, :, part], preferred_element_type=jnp.float32
        )
        weight_parts.append(
            lax.psum_scatter(
                rounded_partial(partial_value).astype(jnp.bfloat16),
                "dp",
                scatter_dimension=1,
                tiled=True,
            ).astype(jnp.float32)
        )
    weight_grad = jnp.concatenate(weight_parts, axis=2).reshape(1, hidden_width, quarter)
    hidden_total = jnp.einsum(
        "rd,fd->rf", arrived, gathered_weight, preferred_element_type=jnp.float32
    )
    hidden_grad = hidden_total.astype(jnp.bfloat16).reshape(expert_hidden.shape)
    return (layer_out, prob_grad, hidden_grad, weight_grad)


def solution(mesh):
    placed = (
        P(("dp", "expert"), None),
        P(("dp", "expert"), None),
        P("dp", "expert", None, None, None),
        P("expert", None, "dp"),
        P(("dp", "expert"), None),
    )
    return jax.shard_map(
        shards,
        mesh=mesh,
        in_specs=placed,
        out_specs=(
            P(("dp", "expert"), None),
            P(("dp", "expert"), None),
            P("dp", "expert", None, None, None),
            P("expert", None, "dp"),
        ),
        check_vma=False,
    )
```

```python
import jax
import jax.numpy as jnp
from jax import lax
from jax.sharding import PartitionSpec as P


def rounded_partial(values):
    narrow = lax.optimization_barrier(values.astype(jnp.bfloat16))
    return narrow.astype(jnp.float32)


def shards(expert_ids, route_probs, expert_hidden, down_weight, out_grad):
    tok_count, top_count = expert_ids.shape
    expert_count = lax.axis_size("expert")
    capacity = expert_hidden.shape[3]
    hidden_width = down_weight.shape[1]
    model_width = out_grad.shape[1]
    slot_count = expert_count * capacity
    flat_ids = expert_ids.reshape(-1)
    onehot = (flat_ids[:, None] == jnp.arange(expert_count, dtype=jnp.int32)[None, :]).astype(
        jnp.int32
    )
    earlier = jnp.cumsum(onehot, axis=0) - onehot
    position = jnp.sum(earlier * onehot, axis=1)
    slot_index = flat_ids * capacity + position
    holds = slot_index[None, :] == jnp.arange(slot_count, dtype=jnp.int32)[:, None]
    route_token = jnp.arange(tok_count * top_count, dtype=jnp.int32) // top_count
    slot_token = jnp.sum(jnp.where(holds, route_token[None, :], 0), axis=1)
    slot_prob = jnp.sum(jnp.where(holds, route_probs.reshape(-1)[None, :], jnp.float32(0.0)), axis=1)
    hidden_rows = expert_hidden.reshape(-1, hidden_width)
    lanes = 128
    grad_tiles = out_grad.reshape(tok_count, model_width // lanes, lanes)
    gathered_weight = lax.all_gather(down_weight, "dp", axis=2, tiled=True)[0]
    slot_out = jnp.dot(
        hidden_rows, gathered_weight, preferred_element_type=jnp.float32
    ).astype(jnp.bfloat16)
    outgoing = slot_out.reshape(expert_count, capacity, model_width // lanes, lanes)
    returned = lax.all_to_all(
        outgoing,
        "expert",
        split_axis=0,
        concat_axis=0,
        tiled=True,
    )
    route_out = returned.reshape(slot_count, model_width // lanes, lanes)[slot_index].reshape(
        tok_count, top_count, model_width // lanes, lanes
    ).astype(jnp.float32)
    layer_out = jnp.sum(route_probs[:, :, None, None] * route_out, axis=1)
    layer_out = layer_out.astype(jnp.bfloat16).reshape(tok_count, model_width)
    prob_grad = jnp.sum(
        grad_tiles[:, None].astype(jnp.float32) * route_out, axis=(2, 3)
    )
    shard_count = lax.axis_size("dp")
    quarter = model_width // shard_count
    split = (shard_count, 2, quarter // 2 // lanes, lanes)
    grad_mixed = out_grad.reshape((tok_count,) + split).transpose(0, 2, 1, 3, 4)
    grad_mixed = grad_mixed.reshape(tok_count, model_width // lanes, lanes)
    scaled = (
        slot_prob[:, None, None] * grad_mixed[slot_token].astype(jnp.float32)
    ).astype(jnp.bfloat16)
    arrived = lax.all_to_all(
        scaled.reshape(expert_count, capacity, model_width // lanes, lanes),
        "expert",
        split_axis=0,
        concat_axis=0,
        tiled=True,
    )
    arrived, _ = lax.optimization_barrier((arrived, outgoing))
    arrived = arrived.reshape(slot_count, model_width // lanes, lanes)
    half_tiles = model_width // lanes // 2
    weight_parts = []
    for part in range(2):
        partial_value = jnp.einsum(
            "rf,rjl->fjl",
            hidden_rows,
            arrived[:, part * half_tiles : (part + 1) * half_tiles],
            preferred_element_type=jnp.float32,
        )
        weight_parts.append(
            lax.psum_scatter(
                rounded_partial(partial_value).astype(jnp.bfloat16),
                "dp",
                scatter_dimension=1,
                tiled=True,
            ).astype(jnp.float32)
        )
    weight_grad = jnp.stack(weight_parts, axis=1).reshape(1, hidden_width, quarter)
    weight_mixed = gathered_weight.reshape((hidden_width,) + split).transpose(0, 2, 1, 3, 4)
    weight_mixed = weight_mixed.reshape(hidden_width, model_width // lanes, lanes)
    hidden_total = jnp.einsum(
        "rjl,fjl->rf", arrived, weight_mixed, preferred_element_type=jnp.float32
    )
    hidden_grad = hidden_total.astype(jnp.bfloat16).reshape(expert_hidden.shape)
    return (layer_out, prob_grad, hidden_grad, weight_grad)


def solution(mesh):
    placed = (
        P(("dp", "expert"), None),
        P(("dp", "expert"), None),
        P("dp", "expert", None, None, None),
        P("expert", None, "dp"),
        P(("dp", "expert"), None),
    )
    return jax.shard_map(
        shards,
        mesh=mesh,
        in_specs=placed,
        out_specs=(
            P(("dp", "expert"), None),
            P(("dp", "expert"), None),
            P("dp", "expert", None, None, None),
            P("expert", None, "dp"),
        ),
        check_vma=False,
    )
```

```python
import functools

import jax
import jax.numpy as jnp
from jax import lax
from jax.experimental import pallas as pl
from jax.experimental.pallas import tpu as pltpu
from jax.sharding import PartitionSpec as P


def combine_kernel(top, index_ref, prob_ref, rows_hbm, grad_ref, layer_ref, dots_ref, held, sems):
    routes = held.shape[0]

    def fetch(i):
        return pltpu.make_async_copy(rows_hbm.at[index_ref[i]], held.at[i], sems.at[i])

    def start(i, carry):
        fetch(i).start()
        return carry

    lax.fori_loop(0, routes, start, 0)

    def finish(i, carry):
        fetch(i).wait()
        return carry

    lax.fori_loop(0, routes, finish, 0)

    def token(t, carry):
        grad = grad_ref[t].astype(jnp.float32)
        total = jnp.zeros(grad.shape, jnp.float32)
        for k in range(top):
            row = held[t * top + k].astype(jnp.float32)
            total = total + prob_ref[t * top + k] * row
            dots_ref[t * top + k] = jnp.sum(grad * row, axis=0, keepdims=True)
        layer_ref[t] = total.astype(layer_ref.dtype)
        return carry

    lax.fori_loop(0, grad_ref.shape[0], token, 0)


def combine(slot_index, probs, rows, grad_tiles):
    tokens, tiles, lanes = grad_tiles.shape
    routes = slot_index.shape[0]
    top = routes // tokens
    smem = pl.BlockSpec(memory_space=pltpu.SMEM)
    vmem = pl.BlockSpec(memory_space=pltpu.VMEM)
    layer, dots = pl.pallas_call(
        functools.partial(combine_kernel, top),
        out_shape=(
            jax.ShapeDtypeStruct((tokens, tiles, lanes), jnp.bfloat16),
            jax.ShapeDtypeStruct((routes, 1, lanes), jnp.float32),
        ),
        in_specs=[smem, smem, pl.BlockSpec(memory_space=pl.ANY), vmem],
        out_specs=(vmem, vmem),
        scratch_shapes=[
            pltpu.VMEM((routes, tiles, lanes), rows.dtype),
            pltpu.SemaphoreType.DMA((routes,)),
        ],
    )(slot_index, probs, rows, grad_tiles)
    return layer, jnp.sum(dots, axis=(1, 2)).reshape(tokens, top)


def rounded_partial(values):
    narrow = lax.optimization_barrier(values.astype(jnp.bfloat16))
    return narrow.astype(jnp.float32)


def shards(expert_ids, route_probs, expert_hidden, down_weight, out_grad):
    tok_count, top_count = expert_ids.shape
    expert_count = lax.axis_size("expert")
    capacity = expert_hidden.shape[3]
    hidden_width = down_weight.shape[1]
    model_width = out_grad.shape[1]
    slot_count = expert_count * capacity
    flat_ids = expert_ids.reshape(-1)
    onehot = (flat_ids[:, None] == jnp.arange(expert_count, dtype=jnp.int32)[None, :]).astype(
        jnp.int32
    )
    earlier = jnp.cumsum(onehot, axis=0) - onehot
    position = jnp.sum(earlier * onehot, axis=1)
    slot_index = flat_ids * capacity + position
    holds = slot_index[None, :] == jnp.arange(slot_count, dtype=jnp.int32)[:, None]
    route_token = jnp.arange(tok_count * top_count, dtype=jnp.int32) // top_count
    slot_token = jnp.sum(jnp.where(holds, route_token[None, :], 0), axis=1)
    slot_prob = jnp.sum(jnp.where(holds, route_probs.reshape(-1)[None, :], jnp.float32(0.0)), axis=1)
    hidden_rows = expert_hidden.reshape(-1, hidden_width)
    lanes = 128
    grad_tiles = out_grad.reshape(tok_count, model_width // lanes, lanes)
    gathered_weight = lax.all_gather(down_weight, "dp", axis=2, tiled=True)[0]
    slot_out = jnp.dot(
        hidden_rows, gathered_weight, preferred_element_type=jnp.float32
    ).astype(jnp.bfloat16)
    outgoing = slot_out.reshape(expert_count, capacity, model_width // lanes, lanes)
    returned = lax.all_to_all(
        outgoing,
        "expert",
        split_axis=0,
        concat_axis=0,
        tiled=True,
    )
    layer_out, prob_grad = combine(
        slot_index,
        route_probs.reshape(-1),
        returned.reshape(slot_count, model_width // lanes, lanes),
        grad_tiles,
    )
    layer_out = layer_out.reshape(tok_count, model_width)
    shard_count = lax.axis_size("dp")
    quarter = model_width // shard_count
    split = (shard_count, 2, quarter // 2 // lanes, lanes)
    grad_mixed = out_grad.reshape((tok_count,) + split).transpose(0, 2, 1, 3, 4)
    grad_mixed = grad_mixed.reshape(tok_count, model_width // lanes, lanes)
    scaled = (
        slot_prob[:, None, None] * grad_mixed[slot_token].astype(jnp.float32)
    ).astype(jnp.bfloat16)
    arrived = lax.all_to_all(
        scaled.reshape(expert_count, capacity, model_width // lanes, lanes),
        "expert",
        split_axis=0,
        concat_axis=0,
        tiled=True,
    )
    arrived, _ = lax.optimization_barrier((arrived, outgoing))
    arrived = arrived.reshape(slot_count, model_width // lanes, lanes)
    half_tiles = model_width // lanes // 2
    weight_parts = []
    for part in range(2):
        partial_value = jnp.einsum(
            "rf,rjl->fjl",
            hidden_rows,
            arrived[:, part * half_tiles : (part + 1) * half_tiles],
            preferred_element_type=jnp.float32,
        )
        weight_parts.append(
            lax.psum_scatter(
                rounded_partial(partial_value).astype(jnp.bfloat16),
                "dp",
                scatter_dimension=1,
                tiled=True,
            ).astype(jnp.float32)
        )
    weight_grad = jnp.stack(weight_parts, axis=1).reshape(1, hidden_width, quarter)
    weight_mixed = gathered_weight.reshape((hidden_width,) + split).transpose(0, 2, 1, 3, 4)
    weight_mixed = weight_mixed.reshape(hidden_width, model_width // lanes, lanes)
    hidden_total = jnp.einsum(
        "rjl,fjl->rf", arrived, weight_mixed, preferred_element_type=jnp.float32
    )
    hidden_grad = hidden_total.astype(jnp.bfloat16).reshape(expert_hidden.shape)
    return (layer_out, prob_grad, hidden_grad, weight_grad)


def solution(mesh):
    placed = (
        P(("dp", "expert"), None),
        P(("dp", "expert"), None),
        P("dp", "expert", None, None, None),
        P("expert", None, "dp"),
        P(("dp", "expert"), None),
    )
    return jax.shard_map(
        shards,
        mesh=mesh,
        in_specs=placed,
        out_specs=(
            P(("dp", "expert"), None),
            P(("dp", "expert"), None),
            P("dp", "expert", None, None, None),
            P("expert", None, "dp"),
        ),
        check_vma=False,
    )
```

```python
import jax
import jax.numpy as jnp
from jax import lax
from jax.sharding import PartitionSpec as P


def rounded_partial(values):
    narrow = lax.optimization_barrier(values.astype(jnp.bfloat16))
    return narrow.astype(jnp.float32)


def shards(expert_ids, route_probs, expert_hidden, down_weight, out_grad):
    tok_count, top_count = expert_ids.shape
    expert_count = lax.axis_size("expert")
    capacity = expert_hidden.shape[3]
    hidden_width = down_weight.shape[1]
    model_width = out_grad.shape[1]
    slot_count = expert_count * capacity
    flat_ids = expert_ids.reshape(-1)
    onehot = (flat_ids[:, None] == jnp.arange(expert_count, dtype=jnp.int32)[None, :]).astype(
        jnp.int32
    )
    earlier = jnp.cumsum(onehot, axis=0) - onehot
    position = jnp.sum(earlier * onehot, axis=1)
    slot_index = flat_ids * capacity + position
    holds = slot_index[None, :] == jnp.arange(slot_count, dtype=jnp.int32)[:, None]
    hidden_rows = expert_hidden.reshape(-1, hidden_width)
    lanes = 128
    grad_tiles = out_grad.reshape(tok_count, model_width // lanes, lanes)
    gathered_weight = lax.all_gather(down_weight, "dp", axis=2, tiled=True)[0]
    slot_out = jnp.dot(
        hidden_rows, gathered_weight, preferred_element_type=jnp.float32
    ).astype(jnp.bfloat16)
    outgoing = slot_out.reshape(expert_count, capacity, model_width // lanes, lanes)
    returned = lax.all_to_all(
        outgoing,
        "expert",
        split_axis=0,
        concat_axis=0,
        tiled=True,
    )
    route_out = returned.reshape(slot_count, model_width // lanes, lanes)[slot_index].reshape(
        tok_count, top_count, model_width // lanes, lanes
    ).astype(jnp.float32)
    layer_out = jnp.sum(route_probs[:, :, None, None] * route_out, axis=1)
    layer_out = layer_out.astype(jnp.bfloat16).reshape(tok_count, model_width)
    prob_grad = jnp.sum(
        grad_tiles[:, None].astype(jnp.float32) * route_out, axis=(2, 3)
    )
    shard_count = lax.axis_size("dp")
    quarter = model_width // shard_count
    split = (shard_count, 2, quarter // 2 // lanes, lanes)
    grad_mixed = out_grad.reshape((tok_count,) + split).transpose(0, 2, 1, 3, 4)
    grad_mixed = grad_mixed.reshape(tok_count, model_width).astype(jnp.float32)
    dispatch = jnp.sum(
        jnp.where(
            holds.reshape(slot_count, tok_count, top_count),
            route_probs[None],
            jnp.float32(0.0),
        ),
        axis=2,
    )
    scaled = jnp.dot(dispatch, grad_mixed, precision=lax.Precision.HIGHEST).astype(jnp.bfloat16)
    arrived = lax.all_to_all(
        scaled.reshape(expert_count, capacity, model_width // lanes, lanes),
        "expert",
        split_axis=0,
        concat_axis=0,
        tiled=True,
    )
    arrived, _ = lax.optimization_barrier((arrived, outgoing))
    arrived = arrived.reshape(slot_count, model_width // lanes, lanes)
    half_tiles = model_width // lanes // 2
    weight_parts = []
    for part in range(2):
        partial_value = jnp.einsum(
            "rf,rjl->fjl",
            hidden_rows,
            arrived[:, part * half_tiles : (part + 1) * half_tiles],
            preferred_element_type=jnp.float32,
        )
        weight_parts.append(
            lax.psum_scatter(
                rounded_partial(partial_value).astype(jnp.bfloat16),
                "dp",
                scatter_dimension=1,
                tiled=True,
            ).astype(jnp.float32)
        )
    weight_grad = jnp.stack(weight_parts, axis=1).reshape(1, hidden_width, quarter)
    weight_mixed = gathered_weight.reshape((hidden_width,) + split).transpose(0, 2, 1, 3, 4)
    weight_mixed = weight_mixed.reshape(hidden_width, model_width // lanes, lanes)
    hidden_total = jnp.einsum(
        "rjl,fjl->rf", arrived, weight_mixed, preferred_element_type=jnp.float32
    )
    hidden_grad = hidden_total.astype(jnp.bfloat16).reshape(expert_hidden.shape)
    return (layer_out, prob_grad, hidden_grad, weight_grad)


def solution(mesh):
    placed = (
        P(("dp", "expert"), None),
        P(("dp", "expert"), None),
        P("dp", "expert", None, None, None),
        P("expert", None, "dp"),
        P(("dp", "expert"), None),
    )
    return jax.shard_map(
        shards,
        mesh=mesh,
        in_specs=placed,
        out_specs=(
            P(("dp", "expert"), None),
            P(("dp", "expert"), None),
            P("dp", "expert", None, None, None),
            P("expert", None, "dp"),
        ),
        check_vma=False,
    )
```

```python
import jax
import jax.numpy as jnp
from jax import lax
from jax.sharding import PartitionSpec as P


def rounded_partial(values):
    narrow = lax.optimization_barrier(values.astype(jnp.bfloat16))
    return narrow.astype(jnp.float32)


def shards(expert_ids, route_probs, expert_hidden, down_weight, out_grad):
    tok_count, top_count = expert_ids.shape
    expert_count = lax.axis_size("expert")
    capacity = expert_hidden.shape[3]
    hidden_width = down_weight.shape[1]
    model_width = out_grad.shape[1]
    slot_count = expert_count * capacity
    flat_ids = expert_ids.reshape(-1)
    onehot = (flat_ids[:, None] == jnp.arange(expert_count, dtype=jnp.int32)[None, :]).astype(
        jnp.int32
    )
    earlier = jnp.cumsum(onehot, axis=0) - onehot
    position = jnp.sum(earlier * onehot, axis=1)
    slot_index = flat_ids * capacity + position
    holds = slot_index[None, :] == jnp.arange(slot_count, dtype=jnp.int32)[:, None]
    hidden_rows = expert_hidden.reshape(-1, hidden_width)
    lanes = 128
    shard_count = lax.axis_size("dp")
    quarter = model_width // shard_count
    split = (shard_count, 2, quarter // 2 // lanes, lanes)
    local_halves = down_weight.reshape(hidden_width, 2, quarter // 2)
    gathered_weight = lax.all_gather(local_halves, "dp", axis=2, tiled=False)
    gathered_weight = gathered_weight.reshape(hidden_width, model_width)
    grad_mixed = out_grad.reshape((tok_count,) + split).transpose(0, 2, 1, 3, 4)
    grad_mixed = grad_mixed.reshape(tok_count, model_width // lanes, lanes)
    slot_out = jnp.dot(
        hidden_rows, gathered_weight, preferred_element_type=jnp.float32
    ).astype(jnp.bfloat16)
    outgoing = slot_out.reshape(expert_count, capacity, model_width // lanes, lanes)
    returned = lax.all_to_all(
        outgoing,
        "expert",
        split_axis=0,
        concat_axis=0,
        tiled=True,
    )
    route_out = returned.reshape(slot_count, model_width // lanes, lanes)[slot_index].reshape(
        tok_count, top_count, model_width // lanes, lanes
    ).astype(jnp.float32)
    layer_out = jnp.sum(route_probs[:, :, None, None] * route_out, axis=1)
    layer_out = layer_out.astype(jnp.bfloat16).reshape((tok_count, 2) + split[:1] + split[2:])
    layer_out = layer_out.transpose(0, 2, 1, 3, 4).reshape(tok_count, model_width)
    prob_grad = jnp.sum(
        grad_mixed[:, None].astype(jnp.float32) * route_out, axis=(2, 3)
    )
    grad_flat = grad_mixed.reshape(tok_count, model_width).astype(jnp.float32)
    dispatch = jnp.sum(
        jnp.where(
            holds.reshape(slot_count, tok_count, top_count),
            route_probs[None],
            jnp.float32(0.0),
        ),
        axis=2,
    )
    scaled = jnp.dot(dispatch, grad_flat, precision=lax.Precision.HIGHEST).astype(jnp.bfloat16)
    arrived = lax.all_to_all(
        scaled.reshape(expert_count, capacity, model_width // lanes, lanes),
        "expert",
        split_axis=0,
        concat_axis=0,
        tiled=True,
    )
    arrived, _ = lax.optimization_barrier((arrived, outgoing))
    arrived = arrived.reshape(slot_count, model_width // lanes, lanes)
    half_tiles = model_width // lanes // 2
    weight_parts = []
    for part in range(2):
        partial_value = jnp.einsum(
            "rf,rjl->fjl",
            hidden_rows,
            arrived[:, part * half_tiles : (part + 1) * half_tiles],
            preferred_element_type=jnp.float32,
        )
        weight_parts.append(
            lax.psum_scatter(
                rounded_partial(partial_value).astype(jnp.bfloat16),
                "dp",
                scatter_dimension=1,
                tiled=True,
            ).astype(jnp.float32)
        )
    weight_grad = jnp.stack(weight_parts, axis=1).reshape(1, hidden_width, quarter)
    weight_mixed = gathered_weight.reshape(hidden_width, model_width // lanes, lanes)
    hidden_total = jnp.einsum(
        "rjl,fjl->rf", arrived, weight_mixed, preferred_element_type=jnp.float32
    )
    hidden_grad = hidden_total.astype(jnp.bfloat16).reshape(expert_hidden.shape)
    return (layer_out, prob_grad, hidden_grad, weight_grad)


def solution(mesh):
    placed = (
        P(("dp", "expert"), None),
        P(("dp", "expert"), None),
        P("dp", "expert", None, None, None),
        P("expert", None, "dp"),
        P(("dp", "expert"), None),
    )
    return jax.shard_map(
        shards,
        mesh=mesh,
        in_specs=placed,
        out_specs=(
            P(("dp", "expert"), None),
            P(("dp", "expert"), None),
            P("dp", "expert", None, None, None),
            P("expert", None, "dp"),
        ),
        check_vma=False,
    )
```

```python
import jax
import jax.numpy as jnp
from jax import lax
from jax.sharding import PartitionSpec as P


def rounded_partial(values):
    narrow = lax.optimization_barrier(values.astype(jnp.bfloat16))
    return narrow.astype(jnp.float32)


def shards(expert_ids, route_probs, expert_hidden, down_weight, out_grad):
    tok_count, top_count = expert_ids.shape
    expert_count = lax.axis_size("expert")
    capacity = expert_hidden.shape[3]
    hidden_width = down_weight.shape[1]
    model_width = out_grad.shape[1]
    slot_count = expert_count * capacity
    flat_ids = expert_ids.reshape(-1)
    onehot = (flat_ids[:, None] == jnp.arange(expert_count, dtype=jnp.int32)[None, :]).astype(
        jnp.int32
    )
    earlier = jnp.cumsum(onehot, axis=0) - onehot
    position = jnp.sum(earlier * onehot, axis=1)
    slot_index = flat_ids * capacity + position
    holds = slot_index[None, :] == jnp.arange(slot_count, dtype=jnp.int32)[:, None]
    hidden_rows = expert_hidden.reshape(-1, hidden_width)
    lanes = 128
    shard_count = lax.axis_size("dp")
    quarter = model_width // shard_count
    split = (shard_count, 2, quarter // 2 // lanes, lanes)
    local_halves = down_weight.reshape(hidden_width, 2, quarter // 2)
    gathered_weight = lax.all_gather(local_halves, "dp", axis=2, tiled=False)
    gathered_weight = gathered_weight.reshape(hidden_width, model_width)
    grad_mixed = out_grad.reshape((tok_count,) + split).transpose(0, 2, 1, 3, 4)
    grad_mixed = grad_mixed.reshape(tok_count, model_width // lanes, lanes)
    slot_out = jnp.dot(
        hidden_rows, gathered_weight, preferred_element_type=jnp.float32
    ).astype(jnp.bfloat16)
    outgoing = slot_out.reshape(expert_count, capacity, model_width // lanes, lanes)
    returned = lax.all_to_all(
        outgoing,
        "expert",
        split_axis=0,
        concat_axis=0,
        tiled=True,
    )
    route_rows = returned.reshape(slot_count, model_width // lanes, lanes)[slot_index].reshape(
        tok_count, top_count, model_width // lanes, lanes
    )
    route_out = route_rows.astype(jnp.float32)
    layer_out = jnp.sum(route_probs[:, :, None, None] * route_out, axis=1)
    layer_out = layer_out.astype(jnp.bfloat16).reshape((tok_count, 2) + split[:1] + split[2:])
    layer_out = layer_out.transpose(0, 2, 1, 3, 4).reshape(tok_count, model_width)
    prob_grad = jnp.einsum(
        "tjl,tkjl->tk", grad_mixed, route_rows, preferred_element_type=jnp.float32
    )
    grad_flat = grad_mixed.reshape(tok_count, model_width).astype(jnp.float32)
    dispatch = jnp.sum(
        jnp.where(
            holds.reshape(slot_count, tok_count, top_count),
            route_probs[None],
            jnp.float32(0.0),
        ),
        axis=2,
    )
    scaled = jnp.dot(dispatch, grad_flat, precision=lax.Precision.HIGHEST).astype(jnp.bfloat16)
    arrived = lax.all_to_all(
        scaled.reshape(expert_count, capacity, model_width // lanes, lanes),
        "expert",
        split_axis=0,
        concat_axis=0,
        tiled=True,
    )
    arrived, _ = lax.optimization_barrier((arrived, outgoing))
    arrived = arrived.reshape(slot_count, model_width // lanes, lanes)
    half_tiles = model_width // lanes // 2
    weight_parts = []
    for part in range(2):
        partial_value = jnp.einsum(
            "rf,rjl->fjl",
            hidden_rows,
            arrived[:, part * half_tiles : (part + 1) * half_tiles],
            preferred_element_type=jnp.float32,
        )
        weight_parts.append(
            lax.psum_scatter(
                rounded_partial(partial_value).astype(jnp.bfloat16),
                "dp",
                scatter_dimension=1,
                tiled=True,
            ).astype(jnp.float32)
        )
    weight_grad = jnp.stack(weight_parts, axis=1).reshape(1, hidden_width, quarter)
    weight_mixed = gathered_weight.reshape(hidden_width, model_width // lanes, lanes)
    hidden_total = jnp.einsum(
        "rjl,fjl->rf", arrived, weight_mixed, preferred_element_type=jnp.float32
    )
    hidden_grad = hidden_total.astype(jnp.bfloat16).reshape(expert_hidden.shape)
    return (layer_out, prob_grad, hidden_grad, weight_grad)


def solution(mesh):
    placed = (
        P(("dp", "expert"), None),
        P(("dp", "expert"), None),
        P("dp", "expert", None, None, None),
        P("expert", None, "dp"),
        P(("dp", "expert"), None),
    )
    return jax.shard_map(
        shards,
        mesh=mesh,
        in_specs=placed,
        out_specs=(
            P(("dp", "expert"), None),
            P(("dp", "expert"), None),
            P("dp", "expert", None, None, None),
            P("expert", None, "dp"),
        ),
        check_vma=False,
    )
```

```python
import jax
import jax.numpy as jnp
from jax import lax
from jax.sharding import PartitionSpec as P


def rounded_partial(values):
    narrow = lax.optimization_barrier(values.astype(jnp.bfloat16))
    return narrow.astype(jnp.float32)


def shards(expert_ids, route_probs, expert_hidden, down_weight, out_grad):
    tok_count, top_count = expert_ids.shape
    expert_count = lax.axis_size("expert")
    capacity = expert_hidden.shape[3]
    hidden_width = down_weight.shape[1]
    model_width = out_grad.shape[1]
    slot_count = expert_count * capacity
    flat_ids = expert_ids.reshape(-1)
    onehot = (flat_ids[:, None] == jnp.arange(expert_count, dtype=jnp.int32)[None, :]).astype(
        jnp.int32
    )
    earlier = jnp.cumsum(onehot, axis=0) - onehot
    position = jnp.sum(earlier * onehot, axis=1)
    slot_index = flat_ids * capacity + position
    holds = slot_index[None, :] == jnp.arange(slot_count, dtype=jnp.int32)[:, None]
    hidden_rows = expert_hidden.reshape(-1, hidden_width)
    lanes = 128
    shard_count = lax.axis_size("dp")
    quarter = model_width // shard_count
    split = (shard_count, 2, quarter // 2 // lanes, lanes)
    local_halves = down_weight.reshape(hidden_width, 2, quarter // 2)
    gathered_weight = lax.all_gather(local_halves, "dp", axis=2, tiled=False)
    gathered_weight = gathered_weight.reshape(hidden_width, model_width)
    grad_mixed = out_grad.reshape((tok_count,) + split).transpose(0, 2, 1, 3, 4)
    grad_mixed = grad_mixed.reshape(tok_count, model_width // lanes, lanes)
    slot_out = jnp.dot(
        hidden_rows, gathered_weight, preferred_element_type=jnp.float32
    ).astype(jnp.bfloat16)
    outgoing = slot_out.reshape(expert_count, capacity, model_width // lanes, lanes)
    returned = lax.all_to_all(
        outgoing,
        "expert",
        split_axis=0,
        concat_axis=0,
        tiled=True,
    )
    route_out = returned.reshape(slot_count, model_width // lanes, lanes)[slot_index].reshape(
        tok_count, top_count, model_width // lanes, lanes
    ).astype(jnp.float32)
    layer_out = jnp.sum(route_probs[:, :, None, None] * route_out, axis=1)
    layer_out = layer_out.astype(jnp.bfloat16).reshape((tok_count, 2) + split[:1] + split[2:])
    layer_out = layer_out.transpose(0, 2, 1, 3, 4).reshape(tok_count, model_width)
    prob_grad = jnp.sum(
        grad_mixed[:, None].astype(jnp.float32) * route_out, axis=(2, 3)
    )
    dispatch = jnp.sum(
        jnp.where(
            holds.reshape(slot_count, tok_count, top_count),
            route_probs[None],
            jnp.float32(0.0),
        ),
        axis=2,
    )
    grad_narrow = grad_mixed.reshape(tok_count, model_width)
    pieces = []
    rest = dispatch
    for _ in range(3):
        piece = rest.astype(jnp.bfloat16)
        pieces.append(piece)
        rest = rest - piece.astype(jnp.float32)
    scaled = sum(
        jnp.dot(piece, grad_narrow, preferred_element_type=jnp.float32) for piece in pieces
    ).astype(jnp.bfloat16)
    arrived = lax.all_to_all(
        scaled.reshape(expert_count, capacity, model_width // lanes, lanes),
        "expert",
        split_axis=0,
        concat_axis=0,
        tiled=True,
    )
    arrived, _ = lax.optimization_barrier((arrived, outgoing))
    arrived = arrived.reshape(slot_count, model_width // lanes, lanes)
    half_tiles = model_width // lanes // 2
    weight_parts = []
    for part in range(2):
        partial_value = jnp.einsum(
            "rf,rjl->fjl",
            hidden_rows,
            arrived[:, part * half_tiles : (part + 1) * half_tiles],
            preferred_element_type=jnp.float32,
        )
        weight_parts.append(
            lax.psum_scatter(
                rounded_partial(partial_value).astype(jnp.bfloat16),
                "dp",
                scatter_dimension=1,
                tiled=True,
            ).astype(jnp.float32)
        )
    weight_grad = jnp.stack(weight_parts, axis=1).reshape(1, hidden_width, quarter)
    weight_mixed = gathered_weight.reshape(hidden_width, model_width // lanes, lanes)
    hidden_total = jnp.einsum(
        "rjl,fjl->rf", arrived, weight_mixed, preferred_element_type=jnp.float32
    )
    hidden_grad = hidden_total.astype(jnp.bfloat16).reshape(expert_hidden.shape)
    return (layer_out, prob_grad, hidden_grad, weight_grad)


def solution(mesh):
    placed = (
        P(("dp", "expert"), None),
        P(("dp", "expert"), None),
        P("dp", "expert", None, None, None),
        P("expert", None, "dp"),
        P(("dp", "expert"), None),
    )
    return jax.shard_map(
        shards,
        mesh=mesh,
        in_specs=placed,
        out_specs=(
            P(("dp", "expert"), None),
            P(("dp", "expert"), None),
            P("dp", "expert", None, None, None),
            P("expert", None, "dp"),
        ),
        check_vma=False,
    )
```

```python
import jax
import jax.numpy as jnp
from jax import lax
from jax.sharding import PartitionSpec as P


def rounded_partial(values):
    narrow = lax.optimization_barrier(values.astype(jnp.bfloat16))
    return narrow.astype(jnp.float32)


def shards(expert_ids, route_probs, expert_hidden, down_weight, out_grad):
    tok_count, top_count = expert_ids.shape
    expert_count = lax.axis_size("expert")
    capacity = expert_hidden.shape[3]
    hidden_width = down_weight.shape[1]
    model_width = out_grad.shape[1]
    slot_count = expert_count * capacity
    flat_ids = expert_ids.reshape(-1)
    onehot = (flat_ids[:, None] == jnp.arange(expert_count, dtype=jnp.int32)[None, :]).astype(
        jnp.int32
    )
    earlier = jnp.cumsum(onehot, axis=0) - onehot
    position = jnp.sum(earlier * onehot, axis=1)
    slot_index = flat_ids * capacity + position
    holds = slot_index[None, :] == jnp.arange(slot_count, dtype=jnp.int32)[:, None]
    hidden_rows = expert_hidden.reshape(-1, hidden_width)
    lanes = 128
    shard_count = lax.axis_size("dp")
    quarter = model_width // shard_count
    split = (shard_count, 2, quarter // 2 // lanes, lanes)
    local_halves = down_weight.reshape(hidden_width, 2, quarter // 2)
    gathered_weight = lax.all_gather(local_halves, "dp", axis=2, tiled=False)
    gathered_weight = gathered_weight.reshape(hidden_width, model_width)
    grad_mixed = out_grad.reshape((tok_count,) + split).transpose(0, 2, 1, 3, 4)
    grad_mixed = grad_mixed.reshape(tok_count, model_width // lanes, lanes)
    slot_out = jnp.dot(
        hidden_rows, gathered_weight, preferred_element_type=jnp.float32
    ).astype(jnp.bfloat16)
    outgoing = slot_out.reshape(expert_count, capacity, model_width // lanes, lanes)
    returned = lax.all_to_all(
        outgoing,
        "expert",
        split_axis=0,
        concat_axis=0,
        tiled=True,
    )
    route_out = returned.reshape(slot_count, model_width // lanes, lanes)[slot_index].reshape(
        tok_count, top_count, model_width // lanes, lanes
    ).astype(jnp.float32)
    layer_out = jnp.sum(route_probs[:, :, None, None] * route_out, axis=1)
    layer_out = layer_out.astype(jnp.bfloat16).reshape((tok_count, 2) + split[:1] + split[2:])
    layer_out = layer_out.transpose(0, 2, 1, 3, 4).reshape(tok_count, model_width)
    prob_grad = jnp.sum(
        grad_mixed[:, None].astype(jnp.float32) * route_out, axis=(2, 3)
    )
    grad_flat = grad_mixed.reshape(tok_count, model_width).astype(jnp.float32)
    dispatch = jnp.sum(
        jnp.where(
            holds.reshape(slot_count, tok_count, top_count),
            route_probs[None],
            jnp.float32(0.0),
        ),
        axis=2,
    )
    scaled = jnp.dot(dispatch, grad_flat, precision=lax.Precision.HIGH).astype(jnp.bfloat16)
    arrived = lax.all_to_all(
        scaled.reshape(expert_count, capacity, model_width // lanes, lanes),
        "expert",
        split_axis=0,
        concat_axis=0,
        tiled=True,
    )
    arrived, _ = lax.optimization_barrier((arrived, outgoing))
    arrived = arrived.reshape(slot_count, model_width // lanes, lanes)
    half_tiles = model_width // lanes // 2
    weight_parts = []
    for part in range(2):
        partial_value = jnp.einsum(
            "rf,rjl->fjl",
            hidden_rows,
            arrived[:, part * half_tiles : (part + 1) * half_tiles],
            preferred_element_type=jnp.float32,
        )
        weight_parts.append(
            lax.psum_scatter(
                rounded_partial(partial_value).astype(jnp.bfloat16),
                "dp",
                scatter_dimension=1,
                tiled=True,
            ).astype(jnp.float32)
        )
    weight_grad = jnp.stack(weight_parts, axis=1).reshape(1, hidden_width, quarter)
    weight_mixed = gathered_weight.reshape(hidden_width, model_width // lanes, lanes)
    hidden_total = jnp.einsum(
        "rjl,fjl->rf", arrived, weight_mixed, preferred_element_type=jnp.float32
    )
    hidden_grad = hidden_total.astype(jnp.bfloat16).reshape(expert_hidden.shape)
    return (layer_out, prob_grad, hidden_grad, weight_grad)


def solution(mesh):
    placed = (
        P(("dp", "expert"), None),
        P(("dp", "expert"), None),
        P("dp", "expert", None, None, None),
        P("expert", None, "dp"),
        P(("dp", "expert"), None),
    )
    return jax.shard_map(
        shards,
        mesh=mesh,
        in_specs=placed,
        out_specs=(
            P(("dp", "expert"), None),
            P(("dp", "expert"), None),
            P("dp", "expert", None, None, None),
            P("expert", None, "dp"),
        ),
        check_vma=False,
    )
```

```python
import jax
import jax.numpy as jnp
from jax import lax
from jax.sharding import PartitionSpec as P


def rounded_partial(values):
    narrow = lax.optimization_barrier(values.astype(jnp.bfloat16))
    return narrow.astype(jnp.float32)


def shards(expert_ids, route_probs, expert_hidden, down_weight, out_grad):
    tok_count, top_count = expert_ids.shape
    expert_count = lax.axis_size("expert")
    capacity = expert_hidden.shape[3]
    hidden_width = down_weight.shape[1]
    model_width = out_grad.shape[1]
    slot_count = expert_count * capacity
    flat_ids = expert_ids.reshape(-1)
    onehot = (flat_ids[:, None] == jnp.arange(expert_count, dtype=jnp.int32)[None, :]).astype(
        jnp.int32
    )
    earlier = jnp.cumsum(onehot, axis=0) - onehot
    position = jnp.sum(earlier * onehot, axis=1)
    slot_index = flat_ids * capacity + position
    holds = slot_index[None, :] == jnp.arange(slot_count, dtype=jnp.int32)[:, None]
    hidden_rows = expert_hidden.reshape(-1, hidden_width)
    lanes = 128
    shard_count = lax.axis_size("dp")
    quarter = model_width // shard_count
    split = (shard_count, 2, quarter // 2 // lanes, lanes)
    local_halves = down_weight.reshape(hidden_width, 2, quarter // 2)
    gathered_weight = lax.all_gather(local_halves, "dp", axis=2, tiled=False)
    gathered_weight = gathered_weight.reshape(hidden_width, model_width)
    grad_mixed = out_grad.reshape((tok_count,) + split).transpose(0, 2, 1, 3, 4)
    grad_mixed = grad_mixed.reshape(tok_count, model_width // lanes, lanes)
    slot_out = jnp.dot(
        hidden_rows, gathered_weight, preferred_element_type=jnp.float32
    ).astype(jnp.bfloat16)
    outgoing = slot_out.reshape(expert_count, capacity, model_width // lanes, lanes)
    returned = lax.all_to_all(
        outgoing,
        "expert",
        split_axis=0,
        concat_axis=0,
        tiled=True,
    )
    route_out = returned.reshape(slot_count, model_width // lanes, lanes)[slot_index].reshape(
        tok_count, top_count, model_width // lanes, lanes
    ).astype(jnp.float32)
    layer_out = jnp.sum(route_probs[:, :, None, None] * route_out, axis=1)
    layer_out = layer_out.astype(jnp.bfloat16).reshape((tok_count, 2) + split[:1] + split[2:])
    layer_out = layer_out.transpose(0, 2, 1, 3, 4).reshape(tok_count, model_width)
    prob_grad = jnp.sum(
        grad_mixed[:, None].astype(jnp.float32) * route_out, axis=(2, 3)
    )
    grad_flat = grad_mixed.reshape(tok_count, model_width).astype(jnp.float32)
    dispatch = jnp.sum(
        jnp.where(
            holds.reshape(slot_count, tok_count, top_count),
            route_probs[None],
            jnp.float32(0.0),
        ),
        axis=2,
    )
    scaled = jnp.dot(dispatch, grad_flat, precision=lax.Precision.DEFAULT).astype(jnp.bfloat16)
    arrived = lax.all_to_all(
        scaled.reshape(expert_count, capacity, model_width // lanes, lanes),
        "expert",
        split_axis=0,
        concat_axis=0,
        tiled=True,
    )
    arrived, _ = lax.optimization_barrier((arrived, outgoing))
    arrived = arrived.reshape(slot_count, model_width // lanes, lanes)
    half_tiles = model_width // lanes // 2
    weight_parts = []
    for part in range(2):
        partial_value = jnp.einsum(
            "rf,rjl->fjl",
            hidden_rows,
            arrived[:, part * half_tiles : (part + 1) * half_tiles],
            preferred_element_type=jnp.float32,
        )
        weight_parts.append(
            lax.psum_scatter(
                rounded_partial(partial_value).astype(jnp.bfloat16),
                "dp",
                scatter_dimension=1,
                tiled=True,
            ).astype(jnp.float32)
        )
    weight_grad = jnp.stack(weight_parts, axis=1).reshape(1, hidden_width, quarter)
    weight_mixed = gathered_weight.reshape(hidden_width, model_width // lanes, lanes)
    hidden_total = jnp.einsum(
        "rjl,fjl->rf", arrived, weight_mixed, preferred_element_type=jnp.float32
    )
    hidden_grad = hidden_total.astype(jnp.bfloat16).reshape(expert_hidden.shape)
    return (layer_out, prob_grad, hidden_grad, weight_grad)


def solution(mesh):
    placed = (
        P(("dp", "expert"), None),
        P(("dp", "expert"), None),
        P("dp", "expert", None, None, None),
        P("expert", None, "dp"),
        P(("dp", "expert"), None),
    )
    return jax.shard_map(
        shards,
        mesh=mesh,
        in_specs=placed,
        out_specs=(
            P(("dp", "expert"), None),
            P(("dp", "expert"), None),
            P("dp", "expert", None, None, None),
            P("expert", None, "dp"),
        ),
        check_vma=False,
    )
```
